32 devices in a mesh: groups: 2 (over y), feat: 4 (over z), head: 4 (over x, core).
Axes of the slice: x: 2, y: 2, z: 4, core: 2. Of those that a mesh axis runs over, the one named last changes fastest.
Arguments:
- token_ids: int32 [32], P('groups'), parts along dimension 0, may hold values from 0 to 75967
- embedding: bfloat16 [75968, 5120], P('head', 'feat'), may hold values from -16 to 16
- retained: bfloat16 [2, 32, 8, 8256, 128], P(None, 'groups', 'head', 'feat'), parts along dimension 1, may hold values from -0.29882812 to 0.29882812
- query_weight: bfloat16 [2, 5120, 5120], P(None, 'feat', 'head'), may hold values from -0.078125 to 0.078125
- key_weight: bfloat16 [2, 5120, 1024], P(None, 'feat', 'head'), may hold values from -0.078125 to 0.078125
- value_weight: bfloat16 [2, 5120, 1024], P(None, 'feat', 'head'), may hold values from -0.078125 to 0.078125
- gate_weight: bfloat16 [2, 5120, 8], P(None, 'feat', 'head'), may hold values from -0.078125 to 0.078125
- gate_bias: float32 [2, 8], P(None, 'head'), may hold values from -4 to 3
- norm_gain: float32 [2, 5120], P(None, 'feat'), may hold values from 0.1 to 1.9
- read_gain: float32 [2, 128], replicated, may hold values from 0.1 to 1.9
- out_weight: bfloat16 [2, 5120, 5120], P(None, 'head', 'feat'), may hold values from -0.078125 to 0.078125
Outputs:
- hidden_out: bfloat16 [32, 5120], P('groups', 'feat'), parts along dimension 0
The draws below stay inside these ranges and needn't reach their ends.
There are 2 independent parts, one for each index of `groups`. The reference program is written for one: setup_inputs(seed, part) draws one part's arguments, and reference() takes and returns one part's arrays. A program takes and returns all parts, laid end to end along the dimension named above; an argument that names none is the same for every part. Nothing has to cross between parts.
All inputs are finite; a program needn't handle non-finite values.
Results may differ from the reference program's by a relative error of at most 0.01345.
The reference program's roundings to bfloat16 on the way (of `stream`, `normed` and `mixed`) count: a program that leaves them out, or rounds other values in their place, can miss the bound.
Values may be sent and summed in bfloat16 or wider, within the bound.
A program may use at most 192 MiB of HBM per device.

```python
import math
import jax
import jax.numpy as jnp
import numpy as np
from jax import lax

D = 5120
QH = 40
KVH = 8
HD = 128
VOCAB = 75968
LAYERS = 2
REQ = 16
FEAT = 8256


def draw_embedding(key, part):
    key_base = jax.random.fold_in(key, 11)
    key_rows = jax.random.fold_in(key, 12)
    column = jnp.arange(D, dtype=jnp.float32) / max(D - 1, 1)
    row_scale = jnp.exp(jax.random.uniform(key_rows, (VOCAB, 1), minval=0.0, maxval=math.log(10.0)))
    rising = jnp.exp(math.log(3.0) * column)
    noise = jax.random.normal(key_base, (VOCAB, D))
    return jnp.clip(0.05 * noise * row_scale * rising, -16.0, 16.0).astype(jnp.bfloat16)


def plant(drawn, own_key, smallest, top_value):
    extent = drawn.shape
    index_at = [jax.random.randint(jax.random.fold_in(own_key, axis), (), 0, extent[axis]) for axis in range(len(extent))]
    drawn = drawn.at[tuple(index_at)].set(smallest)
    longest = extent.index(max(extent))
    index_at[longest] = (index_at[longest] + 1) % extent[longest]
    return drawn.at[tuple(index_at)].set(top_value)


def block_levels(rng, shape, cuts, least, top_value):
    def one(axis_at, parts):
        draws = jax.random.uniform(jax.random.fold_in(jax.random.fold_in(rng, 6), axis_at), (parts,), jnp.float32, least / len(cuts), top_value / len(cuts))
        return jnp.repeat(jnp.exp(draws), shape[axis_at] // parts).reshape((-1,) + (1,) * (len(shape) - axis_at - 1))

    loudness = one(*cuts[0])
    for cut in cuts[1:]:
        loudness = loudness * one(*cut)
    return loudness


def scatter_about(own_key, dims, scale, reach, shards=(), kind=jnp.bfloat16):
    factor_of = block_levels(own_key, dims, shards, -0.22, 0.18) if shards else 1.0
    values = jax.random.normal(own_key, dims, jnp.float32) * scale * factor_of
    return jnp.minimum(jnp.maximum(values, -reach), reach).astype(kind)


def setup_inputs(seed: int = 0, part: int = 0) -> dict:
    key_list = jax.random.split(jax.random.key(seed), 12)
    part_keys = jax.random.split(jax.random.fold_in(key_list[11], part), 12)
    return {
        "token_ids": plant(jax.random.randint(part_keys[0], (REQ,), 0, VOCAB), jax.random.fold_in(part_keys[0], 1), 0, VOCAB - 1).astype(jnp.int32),
        "embedding": draw_embedding(jax.random.fold_in(key_list[11], 71), part),
        "retained": scatter_about(part_keys[2], (LAYERS, REQ, KVH, FEAT, HD), 0.05, 0.29882812, ((2, 4), (3, 4))),
        "query_weight": scatter_about(key_list[3], (LAYERS, D, QH * HD), D ** -0.5, 0.078125, ((1, 4), (2, 4))),
        "key_weight": scatter_about(key_list[4], (LAYERS, D, KVH * HD), D ** -0.5, 0.078125, ((1, 4), (2, 4))),
        "value_weight": scatter_about(key_list[5], (LAYERS, D, KVH * HD), D ** -0.5, 0.078125, ((1, 4), (2, 4))),
        "gate_weight": scatter_about(key_list[6], (LAYERS, D, KVH), D ** -0.5, 0.078125, ((1, 4), (2, 4))),
        "gate_bias": jnp.clip(-4.0 + 7.0 * jax.random.uniform(key_list[7], (LAYERS, KVH), jnp.float32) ** block_levels(key_list[7], (LAYERS, KVH), ((1, 4),), -0.2, 0.2), -4.0, 3.0),
        "norm_gain": jnp.clip(1.0 + 0.18 * jax.random.normal(key_list[8], (LAYERS, D), jnp.float32), 0.1, 1.9),
        "read_gain": jnp.clip(1.0 + 0.18 * jax.random.normal(key_list[9], (LAYERS, HD), jnp.float32), 0.1, 1.9),
        "out_weight": scatter_about(key_list[10], (LAYERS, QH * HD, D), (QH * HD) ** -0.5, 0.078125, ((1, 4), (2, 4))),
    }


def reference(token_ids, embedding, retained, query_weight, key_weight, value_weight, gate_weight, gate_bias, norm_gain, read_gain, out_weight):
    pair_left, pair_right = np.triu_indices(HD)
    pair_left = jnp.asarray(pair_left.astype(np.int32))
    pair_right = jnp.asarray(pair_right.astype(np.int32))
    pair_scale = jnp.where(pair_left == pair_right, 1.0, math.sqrt(2.0)).astype(jnp.float32)
    stream = jnp.take(embedding, token_ids, axis=0)
    for layer_index in range(LAYERS):
        stream_wide = stream.astype(jnp.float32)
        sum_sq = lax.optimization_barrier(jnp.sum(stream_wide * stream_wide, axis=-1, keepdims=True))
        normed = (stream_wide * lax.rsqrt(sum_sq / D + 1e-06) * norm_gain[layer_index]).astype(jnp.bfloat16)
        query = jnp.dot(normed, query_weight[layer_index], preferred_element_type=jnp.float32).astype(jnp.bfloat16)
        query = query.reshape(REQ, KVH, QH // KVH, HD)
        key_rows = jnp.dot(normed, key_weight[layer_index], preferred_element_type=jnp.float32).astype(jnp.bfloat16)
        key_rows = key_rows.reshape(REQ, KVH, HD)
        value_rows = jnp.dot(normed, value_weight[layer_index], preferred_element_type=jnp.float32).astype(jnp.bfloat16)
        value_rows = value_rows.reshape(REQ, KVH, HD)
        gate_logit = jnp.dot(normed, gate_weight[layer_index], preferred_element_type=jnp.float32)
        decay_rate = jnp.exp(-jax.nn.softplus(gate_logit + gate_bias[layer_index]))
        query_wide = query.astype(jnp.float32)
        phi_query = (query_wide[..., pair_left] * query_wide[..., pair_right] * pair_scale).astype(jnp.bfloat16)
        key_wide = key_rows.astype(jnp.float32)
        phi_key = (key_wide[..., pair_left] * key_wide[..., pair_right] * pair_scale / HD).astype(jnp.bfloat16)
        history = jnp.einsum('rhgf,rhfe->rhge', phi_query.astype(jnp.float32), retained[layer_index].astype(jnp.float32))
        cross_term = jnp.einsum('rhgf,rhf->rhg', phi_query.astype(jnp.float32), phi_key.astype(jnp.float32))
        readout = decay_rate[:, :, None, None] * history + cross_term[..., None] * value_rows.astype(jnp.float32)[:, :, None, :]
        scaled = readout * lax.rsqrt(lax.optimization_barrier(jnp.mean(readout * readout, axis=-1, keepdims=True)) + 1e-06) * read_gain[layer_index]
        mixed = scaled.astype(jnp.bfloat16).reshape(REQ, QH * HD)
        branch = jnp.dot(mixed, out_weight[layer_index], preferred_element_type=jnp.float32)
        stream = (stream_wide + branch).astype(jnp.bfloat16)
    return stream
```

```python
import functools
import math

import jax
import jax.numpy as jnp
from jax import lax
from jax.experimental import pallas as pl
from jax.experimental.pallas import tpu as pltpu
from jax.sharding import PartitionSpec as P

MESH = pl.DeviceIdType.MESH
F32 = jnp.float32
BF16 = jnp.bfloat16
SEND = jnp.bfloat16


def lookup(ids_ref, table_hbm, picked_ref, rows_buf, row_sem):
    requests, width = picked_ref.shape
    table_rows = table_hbm.shape[0]
    base = lax.axis_index("head") * table_rows
    window = rows_buf.shape[0] // requests
    out_row = lax.broadcasted_iota(jnp.int32, (requests, requests * window), 0)
    column = lax.broadcasted_iota(jnp.int32, (requests, requests * window), 1)
    select = jnp.zeros((requests, requests * window), F32)
    copies = []
    for i in range(requests):
        local = ids_ref[i] - base
        row = jnp.clip(local, 0, table_rows - 1)
        first = pl.multiple_of(jnp.minimum((row // 8) * 8, table_rows - window), 8)
        copy = pltpu.make_async_copy(
            table_hbm.at[pl.ds(first, window)],
            rows_buf.at[pl.ds(i * window, window)],
            row_sem.at[i],
        )
        copy.start()
        copies.append(copy)
        value = jnp.where(local == row, 1.0, 0.0)
        hit = (out_row == i) & (column == i * window + row - first)
        select = jnp.where(hit, value, select)
    for copy in copies:
        copy.wait()
    picked_ref[...] = jnp.dot(
        select.astype(BF16), rows_buf[...], preferred_element_type=F32
    ).astype(BF16)


def partner_of(me, count, turn):
    if count == 4:
        return (3 - me, lax.rem(me + 2, 4), me + 1 - 2 * lax.rem(me, 2))[turn - 1]
    return lax.rem(me + turn, count)


def kernel(
    feat_count,
    head_count,
    picked_ref,
    retained_hbm,
    query_hbm,
    key_hbm,
    value_hbm,
    gate_hbm,
    bias_ref,
    gain_ref,
    read_ref,
    out_hbm,
    result_ref,
    state,
    query_w,
    key_w,
    value_w,
    gate_w,
    out_w,
    pick_buf,
    query_buf,
    pair_buf,
    small_buf,
    read_buf,
    branch_buf,
    left_sel,
    right_sel,
    pair_scale,
    phi,
    history,
    partial,
    load_sem,
    state_sem,
    send_sem,
    recv_sem,
):
    layers, requests, heads, block, head_size = state.shape
    width = query_w.shape[1]
    query_columns = query_w.shape[2]
    kv_columns = key_w.shape[2]
    chunks, chunk = branch_buf.shape[1], branch_buf.shape[4]
    group = query_columns // (heads * head_size)
    me_feat = lax.axis_index("feat")
    me_head = lax.axis_index("head")

    loads = []
    for layer in range(layers):
        pairs = [(gate_hbm, gate_w), (query_hbm, query_w), (key_hbm, key_w), (value_hbm, value_w)]
        for slot, (source, target) in enumerate(pairs):
            copy = pltpu.make_async_copy(
                source.at[layer], target.at[layer], load_sem.at[layer, slot]
            )
            copy.start()
            loads.append((layer, slot, copy))
        for r in range(requests):
            pltpu.make_async_copy(
                retained_hbm.at[layer, r], state.at[layer, r], state_sem.at[layer, r]
            ).start()
        copy = pltpu.make_async_copy(out_hbm.at[layer], out_w.at[layer], load_sem.at[layer, 4])
        copy.start()
        loads.append((layer, 4, copy))
    load = {(layer, slot): copy for layer, slot, copy in loads}

    barrier = pltpu.get_barrier_semaphore()
    for axis, count, me in (("feat", feat_count, me_feat), ("head", head_count, me_head)):
        for d in range(1, count):
            pl.semaphore_signal(
                barrier, inc=1, device_id={axis: lax.rem(me + d, count)}, device_id_type=MESH
            )
    pl.semaphore_wait(barrier, feat_count + head_count - 2)

    used = [0]

    def exchange(axis, count, me, source_of, target):
        copies = []
        for d in range(1, count):
            copy = pltpu.make_async_remote_copy(
                src_ref=source_of,
                dst_ref=target,
                send_sem=send_sem.at[used[0]],
                recv_sem=recv_sem.at[used[0]],
                device_id={axis: partner_of(me, count, d)},
                device_id_type=MESH,
            )
            copy.start()
            copies.append(copy)
            used[0] += 1
        return copies

    pending = exchange("head", head_count, me_head, picked_ref, pick_buf.at[me_head])
    pick_buf[me_head] = picked_ref[...]

    feature = lax.broadcasted_iota(jnp.int32, (head_size, block), 1) + me_feat * block
    position = lax.broadcasted_iota(jnp.int32, (head_size, block), 0)
    begin = position * head_size - (position * (position - 1)) // 2
    inside = (feature >= begin) & (feature < begin + head_size - position)
    left_sel[...] = jnp.where(inside, 1.0, 0.0).astype(BF16)
    partner = jnp.sum(jnp.where(inside, feature - begin + position, 0), axis=0, keepdims=True)
    right_sel[...] = jnp.where(position == partner, 1.0, 0.0).astype(BF16)
    first = jnp.sum(jnp.where(inside, position, 0), axis=0, keepdims=True)
    pair_scale[...] = jnp.where(first == partner, 1.0, math.sqrt(2.0)).astype(F32)

    slots = requests * 8
    compact = requests * group
    span = group * head_size
    unroll = 4 if requests % 4 == 0 else 1

    def place(rows, columns, swap):
        a = lax.broadcasted_iota(jnp.int32, (rows, columns), 0)
        b = lax.broadcasted_iota(jnp.int32, (rows, columns), 1)
        wide, packed = (b, a) if swap else (a, b)
        match = (packed == (wide % 8) * requests + wide // 8) & (wide % 8 < group)
        return jnp.where(match, 1.0, 0.0).astype(BF16)

    spread = place(slots, compact, False)
    gather = place(compact, slots, True)

    for copy in pending:
        copy.wait()
    stream = pick_buf[0].astype(F32)
    for i in range(1, head_count):
        stream = stream + pick_buf[i].astype(F32)

    for layer in range(layers):
        gained = (stream * gain_ref[layer : layer + 1, :]).astype(BF16)
        square = jnp.sum(stream * stream, axis=1, keepdims=True)
        load[layer, 0].wait()
        gained_wide = gained.astype(F32)
        gates = gate_w[layer].astype(F32)
        lane = lax.broadcasted_iota(jnp.int32, (requests, 128), 1)
        small = jnp.where(lane == heads, square, 0.0)
        for h in range(heads):
            along = jnp.sum(gained_wide * gates[h : h + 1, :], axis=1, keepdims=True)
            small = jnp.where(lane == h, along, small)
        small_buf[layer, me_feat] = small
        small_copies = exchange(
            "feat", feat_count, me_feat, small_buf.at[layer, me_feat], small_buf.at[layer, me_feat]
        )
        load[layer, 1].wait()
        query_copies = []
        for h in range(heads):
            query_buf[layer, h, me_feat] = jnp.dot(
                gained, query_w[layer, :, h * span : (h + 1) * span], preferred_element_type=F32
            ).astype(SEND)
            own = query_buf.at[layer, h, me_feat]
            query_copies.append(exchange("feat", feat_count, me_feat, own, own))
        for slot, weight in ((2, key_w), (3, value_w)):
            load[layer, slot].wait()
            pair_buf[layer, me_feat, :, (slot - 2) * kv_columns : (slot - 1) * kv_columns] = jnp.dot(
                gained, weight[layer], preferred_element_type=F32
            ).astype(SEND)
        own = pair_buf.at[layer, me_feat]
        pair_copies = exchange("feat", feat_count, me_feat, own, own)
        for copy in small_copies:
            copy.wait()
        totals = small_buf[layer, 0]
        for i in range(1, feat_count):
            totals = totals + small_buf[layer, i]
        inverse = lax.rsqrt(totals[:, heads : heads + 1] / (width * feat_count) + 1e-06)
        gate = totals[:, :heads] * inverse + bias_ref[layer : layer + 1, :]
        decay = 1.0 / (1.0 + jnp.exp(gate))
        query = []
        read_copies = []
        for h in range(heads):
            for copy in query_copies[h]:
                copy.wait()
            summed = query_buf[layer, h, 0].astype(F32)
            for i in range(1, feat_count):
                summed = summed + query_buf[layer, h, i].astype(F32)
            summed = (summed * inverse).astype(BF16)
            rows = [summed[:, i * head_size : (i + 1) * head_size] for i in range(group)]
            query.append(rows)
            stacked = jnp.concatenate(rows, axis=0)
            placed = jnp.dot(spread, stacked, preferred_element_type=F32).astype(BF16)
            for start in range(0, block, 256):
                stop = min(start + 256, block)
                left = jnp.dot(placed, left_sel[:, start:stop], preferred_element_type=F32)
                right = jnp.dot(placed, right_sel[:, start:stop], preferred_element_type=F32)
                phi[:, start:stop] = left * right * pair_scale[:, start:stop]

            def read(step, carry, h=h):
                for extra in range(unroll):
                    r = step * unroll + extra
                    if h == 0:
                        pltpu.make_async_copy(
                            retained_hbm.at[layer, r], state.at[layer, r], state_sem.at[layer, r]
                        ).wait()
                for extra in range(unroll):
                    r = step * unroll + extra
                    at = pl.ds(pl.multiple_of(r * 8, 8), 8)
                    history[at, :] = jnp.dot(
                        phi[at, :].astype(BF16), state[layer, r, h], preferred_element_type=F32
                    )
                return carry

            lax.fori_loop(0, requests // unroll, read, 0)
            packed = jnp.dot(gather, history[...].astype(BF16), preferred_element_type=F32)
            read_buf[layer, h, me_feat] = packed.astype(SEND)
            own = read_buf.at[layer, h, me_feat]
            read_copies.append(exchange("feat", feat_count, me_feat, own, own))
        for copy in pair_copies:
            copy.wait()
        summed = pair_buf[layer, 0].astype(F32)
        for i in range(1, feat_count):
            summed = summed + pair_buf[layer, i].astype(F32)
        summed = (summed * inverse).astype(BF16).astype(F32)
        branch_copies = []
        load[layer, 4].wait()
        for h in range(heads):
            key = summed[:, h * head_size : (h + 1) * head_size]
            value = summed[:, kv_columns + h * head_size : kv_columns + (h + 1) * head_size]
            cross = []
            for i in range(group):
                along = jnp.sum(query[h][i].astype(F32) * key, axis=1, keepdims=True)
                cross.append(along * along / head_size)
            for copy in read_copies[h]:
                copy.wait()
            reads = read_buf[layer, h, 0].astype(F32)
            for i in range(1, feat_count):
                reads = reads + read_buf[layer, h, i].astype(F32)
            mixed = []
            for i in range(group):
                readout = (
                    decay[:, h : h + 1] * reads[i * requests : (i + 1) * requests]
                    + cross[i] * value
                )
                scale = lax.rsqrt(jnp.mean(readout * readout, axis=1, keepdims=True) + 1e-06)
                mixed.append((readout * scale * read_ref[layer : layer + 1, :]).astype(BF16))
            mixed = jnp.concatenate(mixed, axis=1)
            for c in range(chunks):
                columns = slice(c * chunk, (c + 1) * chunk)
                part = jnp.dot(
                    mixed,
                    out_w[layer, h * span : (h + 1) * span, columns],
                    preferred_element_type=F32,
                )
                if h > 0:
                    part = part + partial[:, columns]
                if h < heads - 1:
                    partial[:, columns] = part
                else:
                    branch_buf[layer, c, me_head] = part.astype(SEND)
                    own = branch_buf.at[layer, c, me_head]
                    branch_copies.append(exchange("head", head_count, me_head, own, own))
        branch = []
        for c in range(chunks):
            for copy in branch_copies[c]:
                copy.wait()
            total = branch_buf[layer, c, 0].astype(F32)
            for i in range(1, head_count):
                total = total + branch_buf[layer, c, i].astype(F32)
            branch.append(total)
        branch = jnp.concatenate(branch, axis=1) if chunks > 1 else branch[0]
        stream_out = (stream + branch).astype(BF16)
        stream = stream_out.astype(F32)
    result_ref[...] = stream_out


def body(
    feat_count,
    head_count,
    token_ids,
    embedding,
    retained,
    query_weight,
    key_weight,
    value_weight,
    gate_weight,
    gate_bias,
    norm_gain,
    read_gain,
    out_weight,
):
    layers, requests, heads, block, head_size = retained.shape
    width = query_weight.shape[1]
    query_columns = query_weight.shape[2]
    kv_columns = key_weight.shape[2]
    group = query_columns // (heads * head_size)
    chunks = 2 if width % 256 == 0 else 1
    copies = (head_count - 1) + layers * (
        (2 + 2 * heads) * (feat_count - 1) + chunks * (head_count - 1)
    )
    gate_rows = jnp.swapaxes(gate_weight, 1, 2)
    window = 16
    picked = pl.pallas_call(
        lookup,
        out_shape=jax.ShapeDtypeStruct((requests, width), BF16),
        in_specs=[pl.BlockSpec(memory_space=pltpu.SMEM), pl.BlockSpec(memory_space=pl.ANY)],
        out_specs=pl.BlockSpec(memory_space=pltpu.VMEM),
        scratch_shapes=[
            pltpu.VMEM((requests * window, width), BF16),
            pltpu.SemaphoreType.DMA((requests,)),
        ],
    )(token_ids, embedding)
    anywhere = pl.BlockSpec(memory_space=pl.ANY)
    local = pl.BlockSpec(memory_space=pltpu.VMEM)
    return pl.pallas_call(
        functools.partial(kernel, feat_count, head_count),
        out_shape=jax.ShapeDtypeStruct((requests, width), BF16),
        in_specs=[local] + [anywhere] * 5 + [local] * 3 + [anywhere],
        out_specs=local,
        scratch_shapes=[
            pltpu.VMEM(retained.shape, BF16),
            pltpu.VMEM(query_weight.shape, BF16),
            pltpu.VMEM(key_weight.shape, BF16),
            pltpu.VMEM(value_weight.shape, BF16),
            pltpu.VMEM(gate_rows.shape, BF16),
            pltpu.VMEM(out_weight.shape, BF16),
            pltpu.VMEM((head_count, requests, width), BF16),
            pltpu.VMEM((layers, heads, feat_count, requests, group * head_size), SEND),
            pltpu.VMEM((layers, feat_count, requests, 2 * kv_columns), SEND),
            pltpu.VMEM((layers, feat_count, requests, 128), F32),
            pltpu.VMEM((layers, heads, feat_count, requests * group, head_size), SEND),
            pltpu.VMEM((layers, chunks, head_count, requests, width // chunks), SEND),
            pltpu.VMEM((head_size, block), BF16),
            pltpu.VMEM((head_size, block), BF16),
            pltpu.VMEM((1, block), F32),
            pltpu.VMEM((requests * 8, block), F32),
            pltpu.VMEM((requests * 8, head_size), F32),
            pltpu.VMEM((requests, width), F32),
            pltpu.SemaphoreType.DMA((layers, 5)),
            pltpu.SemaphoreType.DMA((layers, requests)),
            pltpu.SemaphoreType.DMA((copies,)),
            pltpu.SemaphoreType.DMA((copies,)),
        ],
        compiler_params=pltpu.CompilerParams(
            collective_id=0, has_side_effects=True, vmem_limit_bytes=66_000_000
        ),
    )(
        picked,
        retained,
        query_weight,
        key_weight,
        value_weight,
        gate_rows,
        gate_bias,
        norm_gain,
        read_gain,
        out_weight,
    )


def solution(mesh):
    return jax.shard_map(
        functools.partial(body, mesh.shape["feat"], mesh.shape["head"]),
        mesh=mesh,
        in_specs=(
            P("groups"),
            P("head", "feat"),
            P(None, "groups", "head", "feat", None),
            P(None, "feat", "head"),
            P(None, "feat", "head"),
            P(None, "feat", "head"),
            P(None, "feat", "head"),
            P(None, "head"),
            P(None, "feat"),
            P(),
            P(None, "head", "feat"),
        ),
        out_specs=P("groups", "feat"),
        check_vma=False,
    )
```

```python
import functools
import math

import jax
import jax.numpy as jnp
from jax import lax
from jax.experimental import pallas as pl
from jax.experimental.pallas import tpu as pltpu
from jax.sharding import PartitionSpec as P

MESH = pl.DeviceIdType.MESH
F32 = jnp.float32
BF16 = jnp.bfloat16
SEND = jnp.bfloat16


def lookup(ids_ref, table_hbm, picked_ref, rows_buf, row_sem):
    requests, width = picked_ref.shape
    table_rows = table_hbm.shape[0]
    base = lax.axis_index("head") * table_rows
    window = rows_buf.shape[0] // requests
    out_row = lax.broadcasted_iota(jnp.int32, (requests, requests * window), 0)
    column = lax.broadcasted_iota(jnp.int32, (requests, requests * window), 1)
    select = jnp.zeros((requests, requests * window), F32)
    copies = []
    for i in range(requests):
        local = ids_ref[i] - base
        row = jnp.clip(local, 0, table_rows - 1)
        first = pl.multiple_of(jnp.minimum((row // 8) * 8, table_rows - window), 8)
        copy = pltpu.make_async_copy(
            table_hbm.at[pl.ds(first, window)],
            rows_buf.at[pl.ds(i * window, window)],
            row_sem.at[i],
        )
        copy.start()
        copies.append(copy)
        value = jnp.where(local == row, 1.0, 0.0)
        hit = (out_row == i) & (column == i * window + row - first)
        select = jnp.where(hit, value, select)
    for copy in copies:
        copy.wait()
    picked_ref[...] = jnp.dot(
        select.astype(BF16), rows_buf[...], preferred_element_type=F32
    ).astype(BF16)


def partner_of(me, count, turn):
    if count == 4:
        return (3 - me, lax.rem(me + 2, 4), me + 1 - 2 * lax.rem(me, 2))[turn - 1]
    return lax.rem(me + turn, count)


def kernel(
    feat_count,
    head_count,
    picked_ref,
    retained_hbm,
    query_hbm,
    key_hbm,
    value_hbm,
    gate_hbm,
    bias_ref,
    gain_ref,
    read_ref,
    out_hbm,
    result_ref,
    state,
    query_w,
    key_w,
    value_w,
    gate_w,
    out_w,
    pick_buf,
    query_buf,
    pair_buf,
    small_buf,
    read_buf,
    branch_buf,
    left_sel,
    right_sel,
    pair_scale,
    phi,
    history,
    partial,
    load_sem,
    state_sem,
    send_sem,
    recv_sem,
):
    layers, requests, heads, block, head_size = state.shape
    width = query_w.shape[1]
    query_columns = query_w.shape[2]
    kv_columns = key_w.shape[2]
    chunks, chunk = branch_buf.shape[1], branch_buf.shape[4]
    group = query_columns // (heads * head_size)
    me_feat = lax.axis_index("feat")
    me_head = lax.axis_index("head")

    load = {}

    def load_inputs(layer):
        pairs = [(gate_hbm, gate_w), (query_hbm, query_w), (key_hbm, key_w), (value_hbm, value_w)]
        for slot, (source, target) in enumerate(pairs):
            load[layer, slot] = pltpu.make_async_copy(
                source.at[layer], target.at[layer], load_sem.at[layer, slot]
            )
            load[layer, slot].start()

    def load_state(layer):
        for r in range(requests):
            pltpu.make_async_copy(
                retained_hbm.at[layer, r], state.at[layer, r], state_sem.at[layer, r]
            ).start()
        load[layer, 4] = pltpu.make_async_copy(
            out_hbm.at[layer], out_w.at[layer], load_sem.at[layer, 4]
        )
        load[layer, 4].start()

    load_inputs(0)

    barrier = pltpu.get_barrier_semaphore()
    for axis, count, me in (("feat", feat_count, me_feat), ("head", head_count, me_head)):
        for d in range(1, count):
            pl.semaphore_signal(
                barrier, inc=1, device_id={axis: lax.rem(me + d, count)}, device_id_type=MESH
            )
    pl.semaphore_wait(barrier, feat_count + head_count - 2)

    used = [0]

    def exchange(axis, count, me, source_of, target):
        copies = []
        for d in range(1, count):
            copy = pltpu.make_async_remote_copy(
                src_ref=source_of,
                dst_ref=target,
                send_sem=send_sem.at[used[0]],
                recv_sem=recv_sem.at[used[0]],
                device_id={axis: partner_of(me, count, d)},
                device_id_type=MESH,
            )
            copy.start()
            copies.append(copy)
            used[0] += 1
        return copies

    pending = exchange("head", head_count, me_head, picked_ref, pick_buf.at[me_head])
    load_state(0)
    pick_buf[me_head] = picked_ref[...]

    feature = lax.broadcasted_iota(jnp.int32, (head_size, block), 1) + me_feat * block
    position = lax.broadcasted_iota(jnp.int32, (head_size, block), 0)
    begin = position * head_size - (position * (position - 1)) // 2
    inside = (feature >= begin) & (feature < begin + head_size - position)
    left_sel[...] = jnp.where(inside, 1.0, 0.0).astype(BF16)
    partner = jnp.sum(jnp.where(inside, feature - begin + position, 0), axis=0, keepdims=True)
    right_sel[...] = jnp.where(position == partner, 1.0, 0.0).astype(BF16)
    first = jnp.sum(jnp.where(inside, position, 0), axis=0, keepdims=True)
    pair_scale[...] = jnp.where(first == partner, 1.0, math.sqrt(2.0)).astype(F32)

    slots = requests * 8
    compact = requests * group
    span = group * head_size
    unroll = 4 if requests % 4 == 0 else 1

    def place(rows, columns, swap):
        a = lax.broadcasted_iota(jnp.int32, (rows, columns), 0)
        b = lax.broadcasted_iota(jnp.int32, (rows, columns), 1)
        wide, packed = (b, a) if swap else (a, b)
        match = (packed == (wide % 8) * requests + wide // 8) & (wide % 8 < group)
        return jnp.where(match, 1.0, 0.0).astype(BF16)

    spread = place(slots, compact, False)
    gather = place(compact, slots, True)

    for copy in pending:
        copy.wait()
    stream = pick_buf[0].astype(F32)
    for i in range(1, head_count):
        stream = stream + pick_buf[i].astype(F32)

    for layer in range(layers):
        gained = (stream * gain_ref[layer : layer + 1, :]).astype(BF16)
        square = jnp.sum(stream * stream, axis=1, keepdims=True)
        load[layer, 0].wait()
        gained_wide = gained.astype(F32)
        gates = gate_w[layer].astype(F32)
        lane = lax.broadcasted_iota(jnp.int32, (requests, 128), 1)
        small = jnp.where(lane == heads, square, 0.0)
        for h in range(heads):
            along = jnp.sum(gained_wide * gates[h : h + 1, :], axis=1, keepdims=True)
            small = jnp.where(lane == h, along, small)
        small_buf[layer, me_feat] = small
        small_copies = exchange(
            "feat", feat_count, me_feat, small_buf.at[layer, me_feat], small_buf.at[layer, me_feat]
        )
        load[layer, 1].wait()
        query_copies = []
        for h in range(heads):
            query_buf[layer, h, me_feat] = jnp.dot(
                gained, query_w[layer, :, h * span : (h + 1) * span], preferred_element_type=F32
            ).astype(SEND)
            own = query_buf.at[layer, h, me_feat]
            query_copies.append(exchange("feat", feat_count, me_feat, own, own))
        for slot, weight in ((2, key_w), (3, value_w)):
            load[layer, slot].wait()
            pair_buf[layer, me_feat, :, (slot - 2) * kv_columns : (slot - 1) * kv_columns] = jnp.dot(
                gained, weight[layer], preferred_element_type=F32
            ).astype(SEND)
        own = pair_buf.at[layer, me_feat]
        pair_copies = exchange("feat", feat_count, me_feat, own, own)
        if layer + 1 < layers:
            load_inputs(layer + 1)
            load_state(layer + 1)
        for copy in small_copies:
            copy.wait()
        totals = small_buf[layer, 0]
        for i in range(1, feat_count):
            totals = totals + small_buf[layer, i]
        inverse = lax.rsqrt(totals[:, heads : heads + 1] / (width * feat_count) + 1e-06)
        gate = totals[:, :heads] * inverse + bias_ref[layer : layer + 1, :]
        decay = 1.0 / (1.0 + jnp.exp(gate))
        query = []
        read_copies = []
        for h in range(heads):
            for copy in query_copies[h]:
                copy.wait()
            summed = query_buf[layer, h, 0].astype(F32)
            for i in range(1, feat_count):
                summed = summed + query_buf[layer, h, i].astype(F32)
            summed = (summed * inverse).astype(BF16)
            rows = [summed[:, i * head_size : (i + 1) * head_size] for i in range(group)]
            query.append(rows)
            stacked = jnp.concatenate(rows, axis=0)
            placed = jnp.dot(spread, stacked, preferred_element_type=F32).astype(BF16)
            for start in range(0, block, 256):
                stop = min(start + 256, block)
                left = jnp.dot(placed, left_sel[:, start:stop], preferred_element_type=F32)
                right = jnp.dot(placed, right_sel[:, start:stop], preferred_element_type=F32)
                phi[:, start:stop] = left * right * pair_scale[:, start:stop]

            def read(step, carry, h=h):
                for extra in range(unroll):
                    r = step * unroll + extra
                    if h == 0:
                        pltpu.make_async_copy(
                            retained_hbm.at[layer, r], state.at[layer, r], state_sem.at[layer, r]
                        ).wait()
                for extra in range(unroll):
                    r = step * unroll + extra
                    at = pl.ds(pl.multiple_of(r * 8, 8), 8)
                    history[at, :] = jnp.dot(
                        phi[at, :].astype(BF16), state[layer, r, h], preferred_element_type=F32
                    )
                return carry

            lax.fori_loop(0, requests // unroll, read, 0)
            packed = jnp.dot(gather, history[...].astype(BF16), preferred_element_type=F32)
            read_buf[layer, h, me_feat] = packed.astype(SEND)
            own = read_buf.at[layer, h, me_feat]
            read_copies.append(exchange("feat", feat_count, me_feat, own, own))
        for copy in pair_copies:
            copy.wait()
        summed = pair_buf[layer, 0].astype(F32)
        for i in range(1, feat_count):
            summed = summed + pair_buf[layer, i].astype(F32)
        summed = (summed * inverse).astype(BF16).astype(F32)
        branch_copies = []
        load[layer, 4].wait()
        for h in range(heads):
            key = summed[:, h * head_size : (h + 1) * head_size]
            value = summed[:, kv_columns + h * head_size : kv_columns + (h + 1) * head_size]
            cross = []
            for i in range(group):
                along = jnp.sum(query[h][i].astype(F32) * key, axis=1, keepdims=True)
                cross.append(along * along / head_size)
            for copy in read_copies[h]:
                copy.wait()
            reads = read_buf[layer, h, 0].astype(F32)
            for i in range(1, feat_count):
                reads = reads + read_buf[layer, h, i].astype(F32)
            mixed = []
            for i in range(group):
                readout = (
                    decay[:, h : h + 1] * reads[i * requests : (i + 1) * requests]
                    + cross[i] * value
                )
                scale = lax.rsqrt(jnp.mean(readout * readout, axis=1, keepdims=True) + 1e-06)
                mixed.append((readout * scale * read_ref[layer : layer + 1, :]).astype(BF16))
            mixed = jnp.concatenate(mixed, axis=1)
            for c in range(chunks):
                columns = slice(c * chunk, (c + 1) * chunk)
                part = jnp.dot(
                    mixed,
                    out_w[layer, h * span : (h + 1) * span, columns],
                    preferred_element_type=F32,
                )
                if h > 0:
                    part = part + partial[:, columns]
                if h < heads - 1:
                    partial[:, columns] = part
                else:
                    branch_buf[layer, c, me_head] = part.astype(SEND)
                    own = branch_buf.at[layer, c, me_head]
                    branch_copies.append(exchange("head", head_count, me_head, own, own))
        branch = []
        for c in range(chunks):
            for copy in branch_copies[c]:
                copy.wait()
            total = branch_buf[layer, c, 0].astype(F32)
            for i in range(1, head_count):
                total = total + branch_buf[layer, c, i].astype(F32)
            branch.append(total)
        branch = jnp.concatenate(branch, axis=1) if chunks > 1 else branch[0]
        stream_out = (stream + branch).astype(BF16)
        stream = stream_out.astype(F32)
    result_ref[...] = stream_out


def body(
    feat_count,
    head_count,
    token_ids,
    embedding,
    retained,
    query_weight,
    key_weight,
    value_weight,
    gate_weight,
    gate_bias,
    norm_gain,
    read_gain,
    out_weight,
):
    layers, requests, heads, block, head_size = retained.shape
    width = query_weight.shape[1]
    query_columns = query_weight.shape[2]
    kv_columns = key_weight.shape[2]
    group = query_columns // (heads * head_size)
    chunks = 2 if width % 256 == 0 else 1
    copies = (head_count - 1) + layers * (
        (2 + 2 * heads) * (feat_count - 1) + chunks * (head_count - 1)
    )
    gate_rows = jnp.swapaxes(gate_weight, 1, 2)
    window = 16
    picked = pl.pallas_call(
        lookup,
        out_shape=jax.ShapeDtypeStruct((requests, width), BF16),
        in_specs=[pl.BlockSpec(memory_space=pltpu.SMEM), pl.BlockSpec(memory_space=pl.ANY)],
        out_specs=pl.BlockSpec(memory_space=pltpu.VMEM),
        scratch_shapes=[
            pltpu.VMEM((requests * window, width), BF16),
            pltpu.SemaphoreType.DMA((requests,)),
        ],
    )(token_ids, embedding)
    anywhere = pl.BlockSpec(memory_space=pl.ANY)
    local = pl.BlockSpec(memory_space=pltpu.VMEM)
    return pl.pallas_call(
        functools.partial(kernel, feat_count, head_count),
        out_shape=jax.ShapeDtypeStruct((requests, width), BF16),
        in_specs=[local] + [anywhere] * 5 + [local] * 3 + [anywhere],
        out_specs=local,
        scratch_shapes=[
            pltpu.VMEM(retained.shape, BF16),
            pltpu.VMEM(query_weight.shape, BF16),
            pltpu.VMEM(key_weight.shape, BF16),
            pltpu.VMEM(value_weight.shape, BF16),
            pltpu.VMEM(gate_rows.shape, BF16),
            pltpu.VMEM(out_weight.shape, BF16),
            pltpu.VMEM((head_count, requests, width), BF16),
            pltpu.VMEM((layers, heads, feat_count, requests, group * head_size), SEND),
            pltpu.VMEM((layers, feat_count, requests, 2 * kv_columns), SEND),
            pltpu.VMEM((layers, feat_count, requests, 128), F32),
            pltpu.VMEM((layers, heads, feat_count, requests * group, head_size), SEND),
            pltpu.VMEM((layers, chunks, head_count, requests, width // chunks), SEND),
            pltpu.VMEM((head_size, block), BF16),
            pltpu.VMEM((head_size, block), BF16),
            pltpu.VMEM((1, block), F32),
            pltpu.VMEM((requests * 8, block), F32),
            pltpu.VMEM((requests * 8, head_size), F32),
            pltpu.VMEM((requests, width), F32),
            pltpu.SemaphoreType.DMA((layers, 5)),
            pltpu.SemaphoreType.DMA((layers, requests)),
            pltpu.SemaphoreType.DMA((copies,)),
            pltpu.SemaphoreType.DMA((copies,)),
        ],
        compiler_params=pltpu.CompilerParams(
            collective_id=0, has_side_effects=True, vmem_limit_bytes=66_000_000
        ),
    )(
        picked,
        retained,
        query_weight,
        key_weight,
        value_weight,
        gate_rows,
        gate_bias,
        norm_gain,
        read_gain,
        out_weight,
    )


def solution(mesh):
    return jax.shard_map(
        functools.partial(body, mesh.shape["feat"], mesh.shape["head"]),
        mesh=mesh,
        in_specs=(
            P("groups"),
            P("head", "feat"),
            P(None, "groups", "head", "feat", None),
            P(None, "feat", "head"),
            P(None, "feat", "head"),
            P(None, "feat", "head"),
            P(None, "feat", "head"),
            P(None, "head"),
            P(None, "feat"),
            P(),
            P(None, "head", "feat"),
        ),
        out_specs=P("groups", "feat"),
        check_vma=False,
    )
```
